32 devices in a mesh: wide: 8 (over y, x, core), narrow: 4 (over z).
Axes of the slice: x: 2, y: 2, z: 4, core: 2. Of those that a mesh axis runs over, the one named last changes fastest.
Arguments:
- tokens: bfloat16 [32768, 768], P(('wide', 'narrow')), may hold values from -6 to 6
- out_grad: bfloat16 [32768, 768], P(('wide', 'narrow')), may hold values from -6 to 6
- routes: int32 [32768, 2], P(('wide', 'narrow')), may hold values from 0 to 15, all different within a row; in each aligned block of 1024 rows (0 to 1023, 1024 to 2047, ...) at most 160 rows name the same one
- replay: int32 [32768], P(('wide', 'narrow')), may hold values 0 or 1
- ln1_gain: bfloat16 [768], P(('wide', 'narrow')), may hold values from 0.5 to 1.5
- ln1_bias: bfloat16 [768], P(('wide', 'narrow')), may hold values from -1.75 to 1.75
- w_qkv: bfloat16 [768, 2304], P(('wide', 'narrow')), may hold values from -0.21875 to 0.21875
- w_out: bfloat16 [768, 768], P(('wide', 'narrow')), may hold values from -3 to 3
- ln2_gain: bfloat16 [768], P(('wide', 'narrow')), may hold values from 0.5 to 1.5
- ln2_bias: bfloat16 [768], P(('wide', 'narrow')), may hold values from -0.625 to 0.625
- w_router: bfloat16 [768, 16], P(('wide', 'narrow')), may hold values from -0.15625 to 0.15625
- frozen_in: bfloat16 [8, 768, 3072], P('wide', 'narrow'), may hold values from -0.21875 to 0.21875
- frozen_out: bfloat16 [8, 3072, 768], P('wide', 'narrow'), may hold values from -0.109375 to 0.109375
- new_in: bfloat16 [8, 768, 3072], P('wide', 'narrow'), may hold values from -0.21875 to 0.21875
- new_out: bfloat16 [8, 3072, 768], P('wide', 'narrow'), may hold values from -0.109375 to 0.109375
Outputs:
- block_out: bfloat16 [32768, 768], P(('wide', 'narrow'))
- tokens_grad: float32 [32768, 768], P(('wide', 'narrow'))
- ln1_gain_grad: float32 [768], P(('wide', 'narrow'))
- ln1_bias_grad: float32 [768], P(('wide', 'narrow'))
- w_qkv_grad: float32 [768, 2304], P(('wide', 'narrow'))
- w_out_grad: float32 [768, 768], P(('wide', 'narrow'))
- ln2_gain_grad: float32 [768], P(('wide', 'narrow'))
- ln2_bias_grad: float32 [768], P(('wide', 'narrow'))
- w_router_grad: float32 [768, 16], P(('wide', 'narrow'))
- new_in_grad: float32 [8, 768, 3072], P('wide', 'narrow')
- new_out_grad: float32 [8, 3072, 768], P('wide', 'narrow')
The draws below stay inside these ranges and needn't reach their ends.
Inputs may be any that keep to these rules, and one draw needn't show every extreme that they name: `routes`: the two ids of a row differ. In the rows of one device (aligned blocks of 1024 rows) no expert is named more than 160 times, a bound that some block reaches.
All inputs are finite; a program needn't handle non-finite values. No bound on the sum of `replay` on one device may be relied on, other than what follows from the above.
Results may differ from the reference program's by a relative error of at most 0.017.
Values may be sent and summed in bfloat16 or wider, within the bound.
No kernel may reach another device: no remote copies, remote signals or barrier semaphores. Data moves between devices by JAX's collectives and lax.ppermute only.
A program may use at most 192 MiB of HBM per device.

```python
import math
import jax
import jax.numpy as jnp
import numpy as np
from jax import lax

D = 768
HEADS = 12
HD = 64
FF = 3072
EXP_DEV = 1
SEQ = 1024
TOK_DEV = 1024
TOKENS = 32768
FROZEN = 8
NEW = 8
EXPERTS = 16
CAP = 160
N_WIDE = 8
N_NARROW = 4


def touch_ends(drawn, rng, least, largest):
    longest = drawn.shape.index(max(drawn.shape))
    spots = []
    for shift in (0, 1):
        where = [jax.random.randint(jax.random.fold_in(rng, axis), (), 0, length) for axis, length in enumerate(drawn.shape)]
        where[longest] = (where[longest] + shift) % drawn.shape[longest]
        spots.append(tuple(where))
    return drawn.at[spots[0]].set(least).at[spots[1]].set(largest)


def with_spikes(values, stream_key, source, target, shards_of, factor):
    owner, partner = [(jnp.arange(values.shape[dim]) // (values.shape[dim] // shards_of)).reshape([-1 if axis == dim else 1 for axis in range(values.ndim)]) for dim in (source, target)]
    chosen = jax.random.permutation(stream_key, shards_of)[partner]
    strong = (owner == chosen) | (owner == (partner + shards_of // 2) % shards_of)
    return jnp.where(strong, factor * values, values)


def shard_levels(stream_key, dims, cuts, least, largest):
    level = 1.0
    for axis_at, parts in cuts:
        draws = jax.random.uniform(jax.random.fold_in(jax.random.fold_in(stream_key, 6), axis_at), (parts,), jnp.float32, least / len(cuts), largest / len(cuts))
        level = level * jnp.repeat(jnp.exp(draws), dims[axis_at] // parts).reshape((-1,) + (1,) * (len(dims) - 1 - axis_at))
    return level


def shared_out(key, own, number, rows, count, top, reach, lean):
    order = jax.random.permutation(key, count)
    crowded, common = shares(count, rows * top, reach, lean, True), shares(count, rows * top, reach, lean, False)
    places = jnp.arange(count)

    def named(lengths, turn):
        used = int((lengths > 0).sum())
        fixed = max(1, used // 4)
        moved = fixed + (places - fixed + turn * (used - fixed)) % max(1, count - fixed)
        return jnp.zeros((count,), jnp.int32).at[order[jnp.where(places < fixed, places, moved)]].set(jnp.asarray(lengths, jnp.int32))

    lengths = jnp.where(number % 4 == 0, named(crowded, number // 4), named(common, number - number // 4 - 1))
    mixed = jax.random.permutation(jax.random.fold_in(own, 3), count)
    giver, sink = mixed[0:count // 2 * 2:2], mixed[1:count // 2 * 2:2]
    margin = jnp.minimum(lengths[giver] - 1, reach - lengths[sink]) // 2
    margin = jnp.where((giver == order[0]) | (sink == order[0]) | (lengths[sink] == 0), 0, jnp.maximum(margin, 0))
    moved = jax.random.randint(jax.random.fold_in(own, 4), (count // 2,), 0, 1 << 20) % (margin + 1)
    lengths = lengths.at[giver].add(-moved).at[sink].add(moved)
    members = jnp.searchsorted(jnp.cumsum(lengths), jnp.arange(rows * top), side="right").astype(jnp.int32)
    listing = members.reshape(top, rows).T
    listing = listing[jax.random.permutation(jax.random.fold_in(own, 1), rows)]
    turn = jax.random.randint(jax.random.fold_in(own, 2), (rows, 1), 0, top)
    return jnp.take_along_axis(listing, (jnp.arange(top)[None, :] + turn) % top, axis=1)


def shares(amount, total, bound, skew, full):
    weights = [(1 << 20) // math.isqrt(standing ** skew) + 1 for standing in range(1, amount + 1)]
    largest = bound if full else min(bound, max(-(-total // amount), total * weights[0] // sum(weights)))
    least = 1 if total - largest >= amount - 1 else 0
    counts, spare = [largest] + [least] * (amount - 1), total - largest - least * (amount - 1)
    while spare > 0:
        free = [i for i in range(1, amount) if counts[i] < largest] or [i for i in range(1, amount) if counts[i] < bound]
        pool, remaining = sum([weights[i] for i in free]), spare
        for i in free:
            extra = min(bound - counts[i], max(1, remaining * weights[i] // pool), spare)
            counts[i] = counts[i] + extra
            spare = spare - extra
    return np.array(counts)


def noise(own_key, extent, scale, bound, split=(), kind=jnp.bfloat16):
    drawn = jax.random.normal(own_key, extent, jnp.float32) * scale
    if len(split) > 0:
        drawn = shard_levels(own_key, extent, split, -0.22, 0.18) * drawn
    return jnp.clip(drawn, min=-bound, max=bound).astype(kind)


def noise_with(own_key, shape, spread, bound, cuts, heavy, kind=jnp.bfloat16):
    values = spread * jax.random.normal(own_key, shape, jnp.float32)
    if cuts:
        values = values * shard_levels(own_key, shape, cuts, -0.22, 0.18)
    return jnp.clip(with_spikes(values, jax.random.fold_in(own_key, 3), *heavy), -bound, bound).astype(kind)


def setup_inputs(seed: int = 0) -> dict:
    seeds = jax.random.split(jax.random.key(seed), 16)
    tokens = noise_with(seeds[0], (TOKENS, D), 1.0, 6.0, ((0, 32),), (0, 1, 32, 2.75))
    out_grad = noise(seeds[1], (TOKENS, D), 1.0, 6.0, ((0, 32),))
    routes_keys = jax.random.split(jax.random.fold_in(seeds[2], 1), TOKENS // TOK_DEV)
    routes_turns = jax.random.permutation(jax.random.fold_in(seeds[2], 3), TOKENS // TOK_DEV)
    routes = jax.vmap(lambda own, number: shared_out(jax.random.fold_in(seeds[2], 2), own, number, TOK_DEV, EXPERTS, 2, CAP, 0))(routes_keys, routes_turns).reshape((TOKENS, 2))
    replay = touch_ends((jax.random.randint(seeds[3], (TOKENS,), 0, 4) < 1).astype(jnp.int32), jax.random.fold_in(seeds[3], 1), 0, 1)
    ln1_gain = jnp.clip(1.0 + 0.1 * jax.random.normal(seeds[4], (D,), jnp.float32), 0.5, 1.5).astype(jnp.bfloat16)
    ln1_bias = noise(seeds[5], (D,), 0.3, 1.75, ((0, 32),))
    w_qkv = noise(seeds[6], (D, 3 * D), D ** -0.5, 0.21875, ((0, 32),))
    w_out = noise(seeds[7], (D, D), 4 ** -0.5, 3.0, ((0, 32),))
    ln2_gain = jnp.clip(1.0 + 0.1 * jax.random.normal(seeds[8], (D,), jnp.float32), 0.5, 1.5).astype(jnp.bfloat16)
    ln2_bias = noise(seeds[9], (D,), 0.1, 0.625, ((0, 32),))
    w_router = noise(seeds[10], (D, EXPERTS), (2 * D) ** -0.5, 0.15625, ((0, 32),))
    frozen_in = noise(seeds[11], (FROZEN, D, FF), D ** -0.5, 0.21875, ((0, 8), (1, 4)))
    frozen_out = noise(seeds[12], (FROZEN, FF, D), FF ** -0.5, 0.109375, ((0, 8), (1, 4)))
    new_in = noise(seeds[13], (NEW, D, FF), D ** -0.5, 0.21875, ((0, 8), (1, 4)))
    new_out = noise(seeds[14], (NEW, FF, D), FF ** -0.5, 0.109375, ((0, 8), (1, 4)))
    return dict(tokens=tokens, out_grad=out_grad, routes=routes, replay=replay, ln1_gain=ln1_gain, ln1_bias=ln1_bias, w_qkv=w_qkv, w_out=w_out, ln2_gain=ln2_gain, ln2_bias=ln2_bias, w_router=w_router, frozen_in=frozen_in, frozen_out=frozen_out, new_in=new_in, new_out=new_out)


@jax.custom_vjp
def low(v):
    return lax.optimization_barrier(v.astype(jnp.bfloat16)).astype(jnp.float32)

@jax.custom_vjp
def low_back(v):
    return v

def low_keep(v):
    return (low(v), None)

def low_pass(kept, grad):
    return (grad,)

def back_keep(v):
    return (v, None)

def back_low(kept, grad):
    return (low(grad),)
low.defvjp(low_keep, low_pass)
low_back.defvjp(back_keep, back_low)
EPSILON = 1e-05
SHIFT = 1.0
NEGATIVE = -1e+30

def smooth(values):
    return jax.nn.gelu(values, approximate=True)

def layer_norm(values, gain, bias):
    centered = values - lax.optimization_barrier(jnp.mean(values, axis=-1, keepdims=True))
    inv_std = lax.rsqrt(lax.optimization_barrier(jnp.mean(centered * centered, axis=-1, keepdims=True)) + EPSILON)
    return centered * inv_std * gain + bias

def causal(length):
    places = jnp.arange(length, dtype=jnp.int32)
    return places[:, None] >= places[None, :]

def reference(tokens, out_grad, routes, replay, ln1_gain, ln1_bias, w_qkv, w_out, ln2_gain, ln2_bias, w_router, frozen_in, frozen_out, new_in, new_out):
    high = lax.Precision.HIGHEST
    group_size = 2 * EXP_DEV
    device_count = N_WIDE * N_NARROW
    expert_ids = jnp.arange(EXPERTS, dtype=jnp.int32)
    flat_blocks = routes.reshape(device_count, 2 * TOK_DEV)
    flat_hot = (flat_blocks[:, :, None] == expert_ids).astype(jnp.int32)
    slots = lax.optimization_barrier(jnp.sum((jnp.cumsum(flat_hot, axis=1) - flat_hot) * flat_hot, axis=2))
    buffer_rows = (jnp.arange(device_count, dtype=jnp.int32)[:, None] * CAP + slots).reshape(-1).astype(jnp.int32)
    flat_routes = routes.reshape(-1).astype(jnp.int32)
    route_hot = (routes[:, :, None] == expert_ids).astype(jnp.float32)
    trainable = (routes % group_size >= EXP_DEV).astype(jnp.float32)
    shifts = SHIFT * replay.astype(jnp.float32)[:, None] * trainable
    allowed = causal(SEQ)
    score_scale = HD ** (-0.5)
    frozen_up = frozen_in.astype(jnp.float32).reshape(N_WIDE, EXP_DEV, D, FF)
    frozen_down = frozen_out.astype(jnp.float32).reshape(N_WIDE, EXP_DEV, FF, D)

    def forward(inputs, gain_one, bias_one, qkv_weight, out_weight, gain_two, bias_two, router_weight, new_up, new_down):
        normed_low = low(layer_norm(inputs, gain_one, bias_one))
        qkv_all = low(low_back(jnp.dot(normed_low, qkv_weight, precision=high)))

        def per_sequence(seq_block):
            queries = seq_block[:, :D].reshape(SEQ, HEADS, HD)
            key_rows = seq_block[:, D:2 * D].reshape(SEQ, HEADS, HD)
            value_rows = seq_block[:, 2 * D:].reshape(SEQ, HEADS, HD)
            scores = low_back(jnp.einsum('qhd,khd->hqk', queries, key_rows, precision=high) * score_scale)
            scores = jnp.where(allowed[None], scores, NEGATIVE)
            probs = low(jax.nn.softmax(scores, axis=-1))
            return jnp.einsum('hqk,khd->qhd', probs, value_rows, precision=high).reshape(SEQ, D)
        mixed = lax.map(jax.checkpoint(per_sequence), qkv_all.reshape(-1, SEQ, 3 * D)).reshape(-1, D)
        mixed = low(low_back(mixed))
        after_attn = inputs + low_back(jnp.dot(mixed, out_weight, precision=high))
        routed = low(layer_norm(after_attn, gain_two, bias_two))
        logits = low_back(jnp.dot(routed, router_weight, precision=high))
        picked = lax.optimization_barrier(jnp.sum(route_hot * logits[:, None, :], axis=2)) - shifts
        gates = jax.nn.softmax(picked, axis=1)
        up_all = jnp.concatenate([frozen_up, new_up.reshape(N_WIDE, EXP_DEV, D, FF)], axis=1).reshape(EXPERTS, D, FF)
        down_all = jnp.concatenate([frozen_down, new_down.reshape(N_WIDE, EXP_DEV, FF, D)], axis=1).reshape(EXPERTS, FF, D)
        pairs = jnp.repeat(routed, 2, axis=0)
        buffers = jnp.zeros((EXPERTS, device_count * CAP, D), jnp.float32).at[flat_routes, buffer_rows].add(pairs)
        buffers = low_back(buffers)

        def per_expert(operands):
            rows_in, up_weight, down_weight = operands
            pre_act = low_back(jnp.dot(rows_in, up_weight, precision=high))
            active = low(smooth(pre_act))
            return low(low_back(jnp.dot(active, down_weight, precision=high)))
        expert_out = lax.map(jax.checkpoint(per_expert), (buffers, up_all, down_all))
        picked_rows = expert_out[flat_routes, buffer_rows].reshape(-1, 2, D)
        return after_attn + lax.optimization_barrier(jnp.sum(gates[:, :, None] * picked_rows, axis=1))
    result, pullback = jax.vjp(forward, tokens.astype(jnp.float32), ln1_gain.astype(jnp.float32), ln1_bias.astype(jnp.float32), w_qkv.astype(jnp.float32), w_out.astype(jnp.float32), ln2_gain.astype(jnp.float32), ln2_bias.astype(jnp.float32), w_router.astype(jnp.float32), new_in.astype(jnp.float32), new_out.astype(jnp.float32))
    grads = pullback(out_grad.astype(jnp.float32))
    return (result.astype(jnp.bfloat16), grads[0], grads[1], grads[2], grads[3], grads[4], grads[5], grads[6], grads[7], grads[8], grads[9])
```

```python
import jax
import jax.numpy as jnp
from jax import lax
from jax.experimental import pallas as pl
from jax.experimental.pallas import tpu as pltpu
from jax.sharding import PartitionSpec as P

HEADS = 12
HD = 64
SEQ = 1024
BLK = 256


EPSILON = 1e-05
SHIFT = 1.0
NEGATIVE = -1e30


def smooth(values):
    return jax.nn.gelu(values, approximate=True)


def layer_norm(values, gain, bias):
    centered = values - jnp.mean(values, axis=-1, keepdims=True)
    inv_std = lax.rsqrt(jnp.mean(centered * centered, axis=-1, keepdims=True) + EPSILON)
    normed = centered * inv_std
    return (normed * gain + bias, normed, inv_std)


def norm_back(grad_norm, normed, inv_std, gain):
    scaled = grad_norm * gain
    return inv_std * (
        scaled
        - jnp.mean(scaled, axis=-1, keepdims=True)
        - normed * jnp.mean(scaled * normed, axis=-1, keepdims=True)
    )


def _nt(a,b): return lax.dot_general(a,b,(((1,),(1,)),((),())),preferred_element_type=jnp.float32)
def _tn(a,b): return lax.dot_general(a,b,(((0,),(0,)),((),())),preferred_element_type=jnp.float32)

def attn_fwd_kernel(q_ref,k_ref,v_ref,o_ref,lse_ref):
    hp=pl.program_id(0); S=q_ref.shape[0]
    @pl.when(hp==0)
    def _(): lse_ref[...]=jnp.zeros_like(lse_ref)
    lane=lax.broadcasted_iota(jnp.int32,(BLK,128),1)
    row=lax.broadcasted_iota(jnp.int32,(BLK,BLK),0); col=lax.broadcasted_iota(jnp.int32,(BLK,BLK),1)
    for i in range(S//BLK):
        sl=pl.ds(i*BLK,BLK)
        q=q_ref[sl,:]*jnp.bfloat16(HD**-0.5)
        kw=(i+1)*BLK
        kb=k_ref[0:kw,:]; vb=v_ref[0:kw,:]
        outs=[]; tops=[]
        for h in range(2):
            mine=(lane<HD) if h==0 else (lane>=HD)
            s=_nt(jnp.where(mine,q,jnp.bfloat16(0)),kb)
            diag=jnp.where(row>=col,s[:,kw-BLK:],NEGATIVE)
            s=diag if i==0 else jnp.concatenate([s[:,:kw-BLK],diag],axis=1)
            m=jnp.max(s,axis=1,keepdims=True)
            e=jnp.exp(s-m)
            l=jnp.sum(e,axis=1,keepdims=True)
            outs.append(jnp.dot(e.astype(jnp.bfloat16),vb,preferred_element_type=jnp.float32)/l)
            tops.append(m+jnp.log(l))
        o_ref[sl,:]=jnp.where(lane<HD,outs[0],outs[1]).astype(jnp.bfloat16)
        lse_ref[sl,:]=jnp.where(lane==2*hp,tops[0],jnp.where(lane==2*hp+1,tops[1],lse_ref[sl,:]))

def attn_fwd(qkv):
    S=qkv.shape[0]; D=HEADS*HD; n=D//128
    return pl.pallas_call(attn_fwd_kernel,grid=(n,),
        in_specs=[pl.BlockSpec((S,128),lambda h:(0,h)),pl.BlockSpec((S,128),lambda h:(0,n+h)),pl.BlockSpec((S,128),lambda h:(0,2*n+h))],
        out_specs=[pl.BlockSpec((S,128),lambda h:(0,h)),pl.BlockSpec((S,128),lambda h:(0,0))],
        out_shape=[jax.ShapeDtypeStruct((S,D),jnp.bfloat16),jax.ShapeDtypeStruct((S,128),jnp.float32)],
        name="attn_fwd")(qkv,qkv,qkv)

def attn_bwd_kernel(q_ref,k_ref,v_ref,g_ref,o_ref,lse_ref,out_ref,dq_ref):
    hp=pl.program_id(0); S=q_ref.shape[0]
    lane=lax.broadcasted_iota(jnp.int32,(BLK,128),1)
    krow=lax.broadcasted_iota(jnp.int32,(BLK,BLK),0); qcol=lax.broadcasted_iota(jnp.int32,(BLK,BLK),1)
    q=q_ref[...]*jnp.bfloat16(HD**-0.5)
    g=g_ref[...]
    prod=g.astype(jnp.float32)*o_ref[...].astype(jnp.float32)
    hi=prod.astype(jnp.bfloat16); lo=(prod-hi.astype(jnp.float32)).astype(jnp.bfloat16)
    l8=lax.broadcasted_iota(jnp.int32,(16,128),1); r8=lax.broadcasted_iota(jnp.int32,(16,128),0)
    pick=jnp.where((l8//HD)==r8,1.0,0.0).astype(jnp.bfloat16)
    delta=_nt(pick,hi)+_nt(pick,lo)
    dq_ref[...]=jnp.zeros_like(dq_ref)
    for j in range(S//BLK):
        sl=pl.ds(j*BLK,BLK); q0=j*BLK
        kb=k_ref[sl,:]; vb=v_ref[sl,:]
        qs=q[q0:,:]; gs=g[q0:,:]
        dvs=[];dks=[]
        acc=None
        for h in range(2):
            mine=(lane<HD) if h==0 else (lane>=HD)
            km=jnp.where(mine,kb,jnp.bfloat16(0)); vm=jnp.where(mine,vb,jnp.bfloat16(0))
            st=_nt(km,qs)-lse_ref[pl.ds(2*hp+h,1),q0:]
            diag=jnp.where(qcol>=krow,st[:,:BLK],NEGATIVE)
            st=diag if q0+BLK==S else jnp.concatenate([diag,st[:,BLK:]],axis=1)
            pt=jnp.exp(st)
            dpt=_nt(vm,gs)
            ds=(pt*(dpt-delta[h:h+1,q0:])).astype(jnp.bfloat16)
            dvs.append(jnp.dot(pt.astype(jnp.bfloat16),gs,preferred_element_type=jnp.float32))
            dks.append(jnp.dot(ds,qs,preferred_element_type=jnp.float32))
            t=_tn(ds,km)
            acc=t if acc is None else acc+t
        dq_ref[pl.ds(q0,S-q0),:]+=acc
        out_ref[1,sl,:]=jnp.where(lane<HD,dks[0],dks[1]).astype(jnp.bfloat16)
        out_ref[2,sl,:]=jnp.where(lane<HD,dvs[0],dvs[1]).astype(jnp.bfloat16)
    out_ref[0]=(dq_ref[...]*HD**-0.5).astype(jnp.bfloat16)

def attn_bwd(qkv,g,o,lse_rows):
    S=qkv.shape[0]; D=HEADS*HD; n=D//128
    return pl.pallas_call(attn_bwd_kernel,grid=(n,),
        in_specs=[pl.BlockSpec((S,128),lambda h:(0,h)),pl.BlockSpec((S,128),lambda h:(0,n+h)),pl.BlockSpec((S,128),lambda h:(0,2*n+h)),
                  pl.BlockSpec((S,128),lambda h:(0,h)),pl.BlockSpec((S,128),lambda h:(0,h)),pl.BlockSpec(lse_rows.shape,lambda h:(0,0))],
        out_specs=pl.BlockSpec((3,S,128),lambda h:(0,0,h)),
        out_shape=jax.ShapeDtypeStruct((3,S,D),jnp.bfloat16),
        scratch_shapes=[pltpu.VMEM((S,128),jnp.float32)],
        name="attn_bwd")(qkv,qkv,qkv,g,o,lse_rows)


def expert_list(frozen_part, new_part):
    return [frozen_part[0]] + [new_part[0]]


def expert_forward(rows_in, up_weight, down_weight):
    pre_act = jnp.dot(rows_in, up_weight, preferred_element_type=jnp.float32)
    active = smooth(pre_act).astype(jnp.bfloat16)
    return jnp.dot(active, down_weight, preferred_element_type=jnp.float32).astype(jnp.bfloat16)


def expert_backward(rows_in, grad_in, up_weight, down_weight, with_weights):
    pre_act = jnp.dot(rows_in, up_weight, preferred_element_type=jnp.float32)
    active, smooth_back = jax.vjp(smooth, pre_act)
    active_low = active.astype(jnp.bfloat16)
    grad_active = lax.dot_general(
        grad_in, down_weight, (((1,), (1,)), ((), ())), preferred_element_type=jnp.float32
    )
    grad_pre = smooth_back(grad_active)[0].astype(jnp.bfloat16)
    down_grad = None
    up_grad = None
    if with_weights:
        down_grad = lax.dot_general(
            active_low, grad_in, (((0,), (0,)), ((), ())), preferred_element_type=jnp.float32
        )
        up_grad = lax.dot_general(
            rows_in, grad_pre, (((0,), (0,)), ((), ())), preferred_element_type=jnp.float32
        )
    row_grad = lax.dot_general(
        grad_pre, up_weight, (((1,), (1,)), ((), ())), preferred_element_type=jnp.float32
    ).astype(jnp.bfloat16)
    return (active_low, row_grad, down_grad, up_grad)


def local(
    tokens,
    out_grad,
    routes,
    replay,
    ln1_gain,
    ln1_bias,
    w_qkv,
    w_out,
    ln2_gain,
    ln2_bias,
    w_router,
    frozen_in,
    frozen_out,
    new_in,
    new_out,
):
    dense_full = (
        lax.all_gather(ln1_gain, ("wide", "narrow"), axis=0, tiled=True),
        lax.all_gather(ln1_bias, ("wide", "narrow"), axis=0, tiled=True),
        lax.all_gather(w_qkv, ("wide", "narrow"), axis=0, tiled=True),
        lax.all_gather(w_out, ("wide", "narrow"), axis=0, tiled=True),
        lax.all_gather(ln2_gain, ("wide", "narrow"), axis=0, tiled=True),
        lax.all_gather(ln2_bias, ("wide", "narrow"), axis=0, tiled=True),
        lax.all_gather(w_router, ("wide", "narrow"), axis=0, tiled=True),
    )
    expert_full = (
        lax.all_gather(frozen_in, "narrow", axis=1, tiled=True),
        lax.all_gather(frozen_out, "narrow", axis=1, tiled=True),
        lax.all_gather(new_in, "narrow", axis=1, tiled=True),
        lax.all_gather(new_out, "narrow", axis=1, tiled=True),
    )
    frozen_up, frozen_down, new_up, new_down = expert_full
    tok_rows = tokens.shape[0]
    model_width = tokens.shape[1]
    expert_count = w_router.shape[1]
    frozen_local = frozen_up.shape[0]
    group_size = frozen_local + new_up.shape[0]
    capacity = 5 * tok_rows // (2 * expert_count)
    inputs_full = tokens.astype(jnp.float32)
    hidden_one, normed_one, inv_one = layer_norm(
        inputs_full, dense_full[0].astype(jnp.float32), dense_full[1].astype(jnp.float32)
    )
    normed_low = hidden_one.astype(jnp.bfloat16)
    qkv_low = jnp.dot(normed_low, dense_full[2], preferred_element_type=jnp.float32).astype(
        jnp.bfloat16
    )
    mixed_low, log_totals = attn_fwd(qkv_low)
    log_rows = jnp.transpose(log_totals)[:16]
    after_attn = inputs_full + jnp.dot(mixed_low, dense_full[3], preferred_element_type=jnp.float32)
    hidden_two, normed_two, inv_two = layer_norm(
        after_attn, dense_full[4].astype(jnp.float32), dense_full[5].astype(jnp.float32)
    )
    routed_low = hidden_two.astype(jnp.bfloat16)
    logits = jnp.dot(routed_low, dense_full[6], preferred_element_type=jnp.float32)
    expert_ids = jnp.arange(expert_count, dtype=jnp.int32)
    route_hot = (routes[:, :, None] == expert_ids).astype(jnp.float32)
    trainable = (routes % group_size >= frozen_local).astype(jnp.float32)
    picked = (
        jnp.sum(route_hot * logits[:, None, :], axis=2)
        - SHIFT * replay.astype(jnp.float32)[:, None] * trainable
    )
    gates = jax.nn.softmax(picked, axis=1)
    flat_routes = routes.reshape(-1)
    pair_count = flat_routes.shape[0]
    flat_hot = (flat_routes[:, None] == expert_ids).astype(jnp.int32)
    slot_index = jnp.sum((jnp.cumsum(flat_hot, axis=0) - flat_hot) * flat_hot, axis=1)
    places = flat_routes * capacity + slot_index
    sources = (
        jnp.full((expert_count * capacity,), pair_count, jnp.int32)
        .at[places]
        .set(jnp.arange(pair_count, dtype=jnp.int32))
    )
    token_rows = jnp.where(sources < pair_count, sources // 2, tok_rows)
    routed_ext = jnp.concatenate([routed_low, jnp.zeros((1, model_width), jnp.bfloat16)], axis=0)
    outgoing = jnp.take(routed_ext, token_rows, axis=0).reshape(expert_count, capacity, model_width)
    grad_out = out_grad.astype(jnp.float32)
    grad_branch = (
        (gates[:, :, None] * grad_out[:, None, :])
        .astype(jnp.bfloat16)
        .reshape(pair_count, model_width)
    )
    branch_ext = jnp.concatenate([grad_branch, jnp.zeros((1, model_width), jnp.bfloat16)], axis=0)
    grad_outgoing = jnp.take(branch_ext, sources, axis=0).reshape(
        expert_count, capacity, model_width
    )
    up_list = expert_list(frozen_up, new_up)
    down_list = expert_list(frozen_down, new_down)
    results = []
    input_grads = []
    up_grads = []
    down_grads = []
    arrived = lax.all_to_all(outgoing, "wide", split_axis=0, concat_axis=1, tiled=True)
    for member in range(group_size):
        results.append(expert_forward(arrived[member], up_list[member], down_list[member]))
    returned = lax.all_to_all(jnp.stack(results), "wide", split_axis=1, concat_axis=0, tiled=True)
    grad_arrived = lax.all_to_all(grad_outgoing, "wide", split_axis=0, concat_axis=1, tiled=True)
    again_up = new_up
    again_down = new_down
    up_back = expert_list(frozen_up, again_up)
    down_back = expert_list(frozen_down, again_down)
    for member in range(group_size):
        active_low, row_grad, down_grad, up_grad = expert_backward(
            arrived[member],
            grad_arrived[member],
            up_back[member],
            down_back[member],
            member >= frozen_local,
        )
        input_grads.append(row_grad)
        if member >= frozen_local:
            down_grads.append(down_grad)
            up_grads.append(up_grad)
    sent_back = lax.all_to_all(
        jnp.stack(input_grads), "wide", split_axis=1, concat_axis=0, tiled=True
    )
    picked_rows = jnp.take(returned.reshape(expert_count * capacity, model_width), places, axis=0)
    picked_rows = picked_rows.astype(jnp.float32).reshape(tok_rows, 2, model_width)
    block_out = (after_attn + jnp.sum(gates[:, :, None] * picked_rows, axis=1)).astype(jnp.bfloat16)
    grad_gates = jnp.sum(grad_out[:, None, :] * picked_rows, axis=2)
    grad_rows = jnp.take(sent_back.reshape(expert_count * capacity, model_width), places, axis=0)
    grad_routed = jnp.sum(grad_rows.astype(jnp.float32).reshape(tok_rows, 2, model_width), axis=1)
    back_dense = (dense_full[0], dense_full[2], dense_full[3], dense_full[4], dense_full[6])
    weighted = jnp.sum(gates * grad_gates, axis=1, keepdims=True)
    grad_picked = gates * (grad_gates - weighted)
    grad_logits = jnp.sum(grad_picked[:, :, None] * route_hot, axis=1).astype(jnp.bfloat16)
    router_grad = lax.dot_general(
        routed_low, grad_logits, (((0,), (0,)), ((), ())), preferred_element_type=jnp.float32
    )
    grad_routed = grad_routed + lax.dot_general(
        grad_logits, back_dense[4], (((1,), (1,)), ((), ())), preferred_element_type=jnp.float32
    )
    gain_two_grad = jnp.sum(grad_routed * normed_two, axis=0)
    bias_two_grad = jnp.sum(grad_routed, axis=0)
    grad_after = grad_out + norm_back(
        grad_routed, normed_two, inv_two, back_dense[3].astype(jnp.float32)
    )
    grad_attn = grad_after.astype(jnp.bfloat16)
    out_proj_grad = lax.dot_general(
        mixed_low, grad_attn, (((0,), (0,)), ((), ())), preferred_element_type=jnp.float32
    )
    grad_mixed = lax.dot_general(
        grad_attn, back_dense[2], (((1,), (1,)), ((), ())), preferred_element_type=jnp.float32
    ).astype(jnp.bfloat16)
    parts = attn_bwd(qkv_low, grad_mixed, mixed_low, log_rows)
    grad_qkv = jnp.concatenate([parts[0], parts[1], parts[2]], axis=1)
    qkv_grad = lax.dot_general(
        normed_low, grad_qkv, (((0,), (0,)), ((), ())), preferred_element_type=jnp.float32
    )
    grad_normed = lax.dot_general(
        grad_qkv, back_dense[1], (((1,), (1,)), ((), ())), preferred_element_type=jnp.float32
    )
    gain_one_grad = jnp.sum(grad_normed * normed_one, axis=0)
    bias_one_grad = jnp.sum(grad_normed, axis=0)
    tokens_grad = grad_after + norm_back(
        grad_normed, normed_one, inv_one, back_dense[0].astype(jnp.float32)
    )
    expert_sums = (
        lax.psum_scatter(
            jnp.stack(up_grads).astype(jnp.bfloat16), "narrow", scatter_dimension=1, tiled=True
        ).astype(jnp.float32),
        lax.psum_scatter(
            jnp.stack(down_grads).astype(jnp.bfloat16), "narrow", scatter_dimension=1, tiled=True
        ).astype(jnp.float32),
    )
    dense_sums = (
        lax.psum_scatter(gain_one_grad, ("wide", "narrow"), scatter_dimension=0, tiled=True),
        lax.psum_scatter(bias_one_grad, ("wide", "narrow"), scatter_dimension=0, tiled=True),
        lax.psum_scatter(qkv_grad, ("wide", "narrow"), scatter_dimension=0, tiled=True),
        lax.psum_scatter(out_proj_grad, ("wide", "narrow"), scatter_dimension=0, tiled=True),
        lax.psum_scatter(gain_two_grad, ("wide", "narrow"), scatter_dimension=0, tiled=True),
        lax.psum_scatter(bias_two_grad, ("wide", "narrow"), scatter_dimension=0, tiled=True),
        lax.psum_scatter(router_grad, ("wide", "narrow"), scatter_dimension=0, tiled=True),
    )
    return (
        block_out,
        tokens_grad,
        dense_sums[0],
        dense_sums[1],
        dense_sums[2],
        dense_sums[3],
        dense_sums[4],
        dense_sums[5],
        dense_sums[6],
        expert_sums[0],
        expert_sums[1],
    )


def solution(mesh):
    placed = (
        P(("wide", "narrow"), None),
        P(("wide", "narrow"), None),
        P(("wide", "narrow"), None),
        P(("wide", "narrow")),
        P(("wide", "narrow")),
        P(("wide", "narrow")),
        P(("wide", "narrow"), None),
        P(("wide", "narrow"), None),
        P(("wide", "narrow")),
        P(("wide", "narrow")),
        P(("wide", "narrow"), None),
        P("wide", "narrow", None),
        P("wide", "narrow", None),
        P("wide", "narrow", None),
        P("wide", "narrow", None),
    )
    return jax.shard_map(
        local,
        mesh=mesh,
        in_specs=placed,
        out_specs=(
            P(("wide", "narrow"), None),
            P(("wide", "narrow"), None),
            P(("wide", "narrow")),
            P(("wide", "narrow")),
            P(("wide", "narrow"), None),
            P(("wide", "narrow"), None),
            P(("wide", "narrow")),
            P(("wide", "narrow")),
            P(("wide", "narrow"), None),
            P("wide", "narrow", None),
            P("wide", "narrow", None),
        ),
        check_vma=False,
    )
```
